32 devices in a mesh: groups: 2 (over y), section: 8 (over z, x), sub: 2 (over core).
Axes of the slice: x: 2, y: 2, z: 4, core: 2. Of those that a mesh axis runs over, the one named last changes fastest.
Arguments:
- echoes: float32 [4, 384, 32, 256], P('groups', None, 'section', 'sub'), parts along dimension 0, may hold values from -6 to 6
- range_taps: float32 [2, 5], replicated, may hold values from -3 to 3
- pulse_taper: float32 [256], replicated, may hold values from 0.3 to 1
- channel_phase: float32 [256], replicated, may hold values from -3.140625 to 3.140625
- loading: float32 [1], replicated, may hold values from 0.5 to 2
- beam_index: int32 [256], replicated, may hold values from 0 to 1023
Outputs:
- normalized_beams: float32 [2, 256, 32, 256], P('groups', ('section', 'sub')), parts along dimension 0
The draws below stay inside these ranges and needn't reach their ends.
There are 2 independent parts, one for each index of `groups`. The reference program is written for one: setup_inputs(seed, part) draws one part's arguments, and reference() takes and returns one part's arrays. A program takes and returns all parts, laid end to end along the dimension named above; an argument that names none is the same for every part. Nothing has to cross between parts.
All inputs are finite; a program needn't handle non-finite values. Where the reference program divides by a largest or mean magnitude, that divisor is 1e-20 or more.
Results may differ from the reference program's by a relative error of at most 0.0003.
Values sent between devices are 32-bit elements; how exact they have to be, the bound alone decides.
A program may use at most 64 MiB of HBM per device.

```python
import math
import jax
import jax.numpy as jnp
from jax import lax

CHANNELS = 256
PULSES = 256
BEAMS = 256
INTERVALS = 2
ITERS = 2
LOOKS = 1024
HALF = 2
GATES = 32
HOP = 128
TRAIN = 384


def plant(entries, rng, least, high):
    shape = entries.shape
    place = [jax.random.randint(jax.random.fold_in(rng, axis), (), 0, shape[axis]) for axis in range(len(shape))]
    entries = entries.at[tuple(place)].set(least)
    longest = shape.index(max(shape))
    place[longest] = (place[longest] + 1) % shape[longest]
    return entries.at[tuple(place)].set(high)


def block_levels(stream_key, shape, split, low, largest):
    loudness, own = 1.0, jax.random.fold_in(stream_key, 6)
    for position, parts in split:
        steps = jnp.exp(jax.random.uniform(jax.random.fold_in(own, position), (parts,), jnp.float32, low / len(split), largest / len(split)))
        loudness = loudness * jnp.repeat(steps, shape[position] // parts).reshape([-1 if axis == position else 1 for axis in range(len(shape))])
    return loudness


def noise(stream_key, dims, width, reach, shards=(), kind=jnp.bfloat16):
    drawn = jax.random.normal(stream_key, dims, jnp.float32) * width
    if len(shards) > 0:
        drawn = block_levels(stream_key, dims, shards, -0.22, 0.18) * drawn
    return jnp.clip(drawn, min=-reach, max=reach).astype(kind)


def setup_inputs(seed: int = 0, part: int = 0) -> dict:
    keys = jax.random.split(jax.random.key(seed), 7)
    own_keys = jax.random.split(jax.random.fold_in(keys[6], part), 7)
    return {
        "echoes": noise(own_keys[0], (2, TRAIN, GATES, CHANNELS), 1.0, 6.0, ((2, 8), (3, 2)), jnp.float32),
        "range_taps": noise(keys[1], (2, 2 * HALF + 1), 0.5, 3.0, (), jnp.float32),
        "pulse_taper": jnp.clip(jnp.exp(jax.random.uniform(keys[2], (PULSES,), jnp.float32, math.log(0.3), math.log(1.0))), 0.3, 1.0),
        "channel_phase": jnp.clip(jax.random.uniform(keys[3], (CHANNELS,), jnp.float32, -3.140625, 3.140625), -3.140625, 3.140625),
        "loading": jnp.clip(jnp.exp(jax.random.uniform(keys[4], (1,), jnp.float32, math.log(0.5), math.log(2.0))), 0.5, 2.0),
        "beam_index": plant(jax.random.randint(keys[5], (BEAMS,), 0, LOOKS), jax.random.fold_in(keys[5], 1), 0, LOOKS - 1).astype(jnp.int32),
    }


precise = lax.Precision.HIGHEST
epsilon = 1e-6


def apply_taps(pad_real, pad_imag, range_taps, gate_count):
    axis_gates = pad_real.ndim - 2
    shape_out = pad_real.shape[:axis_gates] + (gate_count,) + pad_real.shape[axis_gates + 1:]
    out_real = jnp.zeros(shape_out, jnp.float32)
    out_imag = jnp.zeros(shape_out, jnp.float32)
    for offset in range(range_taps.shape[1]):
        part_real = lax.slice_in_dim(pad_real, offset, offset + gate_count, axis=axis_gates)
        part_imag = lax.slice_in_dim(pad_imag, offset, offset + gate_count, axis=axis_gates)
        out_real = out_real + range_taps[0, offset] * part_real - range_taps[1, offset] * part_imag
        out_imag = out_imag + range_taps[0, offset] * part_imag + range_taps[1, offset] * part_real
    return out_real, out_imag


def doppler_table(pulse_taper):
    pulse_count = pulse_taper.shape[0]
    pulse_index = jnp.arange(pulse_count, dtype=jnp.int32)
    product = (pulse_index[:, None] * pulse_index[None, :]) % pulse_count
    phase_angle = (2.0 * math.pi / pulse_count) * product.astype(jnp.float32)
    cosine = jnp.cos(phase_angle) * pulse_taper[None, :]
    sine_part = jnp.sin(phase_angle) * pulse_taper[None, :]
    upper_rows = jnp.concatenate([cosine, sine_part], axis=1)
    lower_rows = jnp.concatenate([-sine_part, cosine], axis=1)
    return jnp.concatenate([upper_rows, lower_rows], axis=0)


def transform(doppler, segment):
    shape_in = segment.shape
    flattened = segment.reshape(shape_in[0] * shape_in[1], -1)
    result = jnp.dot(doppler, flattened, precision=precise, preferred_element_type=jnp.float32)
    return result.reshape(shape_in)


def batched(first, second):
    return jnp.einsum('dij,djk->dik', first, second, precision=precise)


def complex_product(left_real, left_imag, right_real, right_imag):
    out_real = batched(left_real, right_real) - batched(left_imag, right_imag)
    out_imag = batched(left_real, right_imag) + batched(left_imag, right_real)
    return out_real, out_imag


def gram_product(first, second):
    return jnp.einsum('dgi,dgj->dij', first, second, precision=precise)


def loaded_inverse(real_part, imag_part, loading):
    gate_count = real_part.shape[1]
    channels = real_part.shape[2]
    cov_real = (gram_product(real_part, real_part) + gram_product(imag_part, imag_part)) / gate_count
    cov_imag = (gram_product(real_part, imag_part) - gram_product(imag_part, real_part)) / gate_count
    identity = jnp.eye(channels, dtype=jnp.float32)
    trace_sum = jnp.sum(cov_real * identity[None], axis=(1, 2))
    cov_real = cov_real + (loading[0] * trace_sum / channels)[:, None, None] * identity[None]
    row_bound = jnp.max(jnp.sum(jnp.abs(cov_real) + jnp.abs(cov_imag), axis=2), axis=1)
    inv_real = identity[None] / row_bound[:, None, None]
    inv_imag = jnp.zeros_like(inv_real)
    for newton_step in range(ITERS):
        prod_real, prod_imag = complex_product(cov_real, cov_imag, inv_real, inv_imag)
        inv_real, inv_imag = complex_product(inv_real, inv_imag, 2.0 * identity[None] - prod_real, -prod_imag)
    return inv_real, inv_imag


def steering(beam_index, channel_phase):
    channels = channel_phase.shape[0]
    direction = -1.0 + (2.0 * beam_index.astype(jnp.float32) + 1.0) / LOOKS
    phase_angle = math.pi * jnp.arange(channels, dtype=jnp.float32)[:, None] * direction[None, :] + channel_phase[:, None]
    return jnp.cos(phase_angle), jnp.sin(phase_angle)


def beam_weights(inv_real, inv_imag, steer_real, steer_imag):
    weight_real = jnp.einsum('dij,jb->dib', inv_real, steer_real, precision=precise) - jnp.einsum('dij,jb->dib', inv_imag, steer_imag, precision=precise)
    weight_imag = jnp.einsum('dij,jb->dib', inv_real, steer_imag, precision=precise) + jnp.einsum('dij,jb->dib', inv_imag, steer_real, precision=precise)
    gain_norm = jnp.sum(steer_real[None] * weight_real + steer_imag[None] * weight_imag, axis=1)
    return weight_real / gain_norm[:, None, :], weight_imag / gain_norm[:, None, :]


def form_beams(data_real, data_imag, weight_real, weight_imag):
    out_real = jnp.einsum('dgc,dcb->dgb', data_real, weight_real, precision=precise) + jnp.einsum('dgc,dcb->dgb', data_imag, weight_imag, precision=precise)
    out_imag = jnp.einsum('dgc,dcb->dgb', data_imag, weight_real, precision=precise) - jnp.einsum('dgc,dcb->dgb', data_real, weight_imag, precision=precise)
    return out_real * out_real + out_imag * out_imag


def reference(echoes, range_taps, pulse_taper, channel_phase, loading, beam_index):
    rim_width = range_taps.shape[1] // 2
    padded = jnp.pad(echoes, ((0, 0), (0, 0), (rim_width, rim_width), (0, 0)))
    filt_real, filt_imag = apply_taps(padded[0], padded[1], range_taps, echoes.shape[2])
    filtered = jnp.stack([filt_real, filt_imag])
    doppler = doppler_table(pulse_taper)
    spectra = [transform(doppler, lax.slice_in_dim(filtered, interval * HOP, interval * HOP + PULSES, axis=1)) for interval in range(INTERVALS)]
    steer_real, steer_imag = steering(beam_index, channel_phase)
    outputs = []
    for interval in range(INTERVALS - 1):
        inv_real, inv_imag = loaded_inverse(spectra[interval][0], spectra[interval][1], loading)
        weight_real, weight_imag = beam_weights(inv_real, inv_imag, steer_real, steer_imag)
        beam_power = form_beams(spectra[interval + 1][0], spectra[interval + 1][1], weight_real, weight_imag)
        noise_level = jnp.sum(beam_power, axis=(0, 1)) / (PULSES * GATES)
        outputs.append(beam_power / (noise_level + epsilon))
    return jnp.stack(outputs)
```

```python
import functools
import math

import jax
import jax.numpy as jnp
import numpy as np
from jax import lax
from jax.experimental import pallas as pl
from jax.experimental.pallas import tpu as pltpu
from jax.sharding import PartitionSpec as P

PULSES = 256
INTERVALS = 2
ITERS = 2
LOOKS = 1024
HOP = 128


precise = lax.Precision.HIGHEST
epsilon = 1e-06


def apply_taps(pad_real, pad_imag, range_taps, gate_count):
    axis_gates = pad_real.ndim - 2
    shape_out = pad_real.shape[:axis_gates] + (gate_count,) + pad_real.shape[axis_gates + 1 :]
    out_real = jnp.zeros(shape_out, jnp.float32)
    out_imag = jnp.zeros(shape_out, jnp.float32)
    for offset in range(range_taps.shape[1]):
        part_real = lax.slice_in_dim(pad_real, offset, offset + gate_count, axis=axis_gates)
        part_imag = lax.slice_in_dim(pad_imag, offset, offset + gate_count, axis=axis_gates)
        out_real = out_real + range_taps[0, offset] * part_real - range_taps[1, offset] * part_imag
        out_imag = out_imag + range_taps[0, offset] * part_imag + range_taps[1, offset] * part_real
    return (out_real, out_imag)


def doppler_table(pulse_taper):
    pulse_count = pulse_taper.shape[0]
    pulse_index = jnp.arange(pulse_count, dtype=jnp.int32)
    product = pulse_index[:, None] * pulse_index[None, :] % pulse_count
    phase_angle = 2.0 * math.pi / pulse_count * product.astype(jnp.float32)
    cosine = jnp.cos(phase_angle) * pulse_taper[None, :]
    sine_part = jnp.sin(phase_angle) * pulse_taper[None, :]
    upper_rows = jnp.concatenate([cosine, sine_part], axis=1)
    lower_rows = jnp.concatenate([-sine_part, cosine], axis=1)
    return jnp.concatenate([upper_rows, lower_rows], axis=0)


def transform(doppler, segment):
    shape_in = segment.shape
    flattened = segment.reshape(shape_in[0] * shape_in[1], -1)
    result = jnp.dot(doppler, flattened, precision=precise, preferred_element_type=jnp.float32)
    return result.reshape(shape_in)


def batched(first, second):
    return jnp.einsum("dij,djk->dik", first, second, precision=precise)


def complex_product(left_real, left_imag, right_real, right_imag):
    out_real = batched(left_real, right_real) - batched(left_imag, right_imag)
    out_imag = batched(left_real, right_imag) + batched(left_imag, right_real)
    return (out_real, out_imag)


def gram_product(first, second):
    return jnp.einsum("dgi,dgj->dij", first, second, precision=precise)


def loaded_inverse(real_part, imag_part, loading):
    gate_count = real_part.shape[1]
    channels = real_part.shape[2]
    cov_real = (
        gram_product(real_part, real_part) + gram_product(imag_part, imag_part)
    ) / gate_count
    cov_imag = (
        gram_product(real_part, imag_part) - gram_product(imag_part, real_part)
    ) / gate_count
    identity = jnp.eye(channels, dtype=jnp.float32)
    trace_sum = jnp.sum(cov_real * identity[None], axis=(1, 2))
    cov_real = cov_real + (loading[0] * trace_sum / channels)[:, None, None] * identity[None]
    row_bound = jnp.max(jnp.sum(jnp.abs(cov_real) + jnp.abs(cov_imag), axis=2), axis=1)
    inv_real = identity[None] / row_bound[:, None, None]
    inv_imag = jnp.zeros_like(inv_real)
    for newton_step in range(ITERS):
        prod_real, prod_imag = complex_product(cov_real, cov_imag, inv_real, inv_imag)
        inv_real, inv_imag = complex_product(
            inv_real, inv_imag, 2.0 * identity[None] - prod_real, -prod_imag
        )
    return (inv_real, inv_imag)


def steering(beam_index, channel_phase):
    channels = channel_phase.shape[0]
    direction = -1.0 + (2.0 * beam_index.astype(jnp.float32) + 1.0) / LOOKS
    phase_angle = (
        math.pi * jnp.arange(channels, dtype=jnp.float32)[:, None] * direction[None, :]
        + channel_phase[:, None]
    )
    return (jnp.cos(phase_angle), jnp.sin(phase_angle))


def beam_weights(inv_real, inv_imag, steer_real, steer_imag):
    weight_real = jnp.einsum("dij,jb->dib", inv_real, steer_real, precision=precise) - jnp.einsum(
        "dij,jb->dib", inv_imag, steer_imag, precision=precise
    )
    weight_imag = jnp.einsum("dij,jb->dib", inv_real, steer_imag, precision=precise) + jnp.einsum(
        "dij,jb->dib", inv_imag, steer_real, precision=precise
    )
    gain_norm = jnp.sum(steer_real[None] * weight_real + steer_imag[None] * weight_imag, axis=1)
    return (weight_real / gain_norm[:, None, :], weight_imag / gain_norm[:, None, :])


def form_beams(data_real, data_imag, weight_real, weight_imag):
    out_real = jnp.einsum("dgc,dcb->dgb", data_real, weight_real, precision=precise) + jnp.einsum(
        "dgc,dcb->dgb", data_imag, weight_imag, precision=precise
    )
    out_imag = jnp.einsum("dgc,dcb->dgb", data_imag, weight_real, precision=precise) - jnp.einsum(
        "dgc,dcb->dgb", data_real, weight_imag, precision=precise
    )
    return out_real * out_real + out_imag * out_imag


def on_device(echoes, range_taps, pulse_taper, channel_phase, loading, beam_index):
    rim_width = range_taps.shape[1] // 2
    doppler = doppler_table(pulse_taper)
    spectra = [
        transform(
            doppler, lax.slice_in_dim(echoes, interval * HOP, interval * HOP + PULSES, axis=1)
        )
        for interval in range(INTERVALS)
    ]
    turned = [
        lax.all_to_all(
            lax.all_to_all(spectrum, "section", split_axis=1, concat_axis=2, tiled=True),
            "sub",
            split_axis=1,
            concat_axis=3,
            tiled=True,
        )
        for spectrum in spectra
    ]
    refined = []
    for spectrum in turned:
        padded_bins = jnp.pad(spectrum, ((0, 0), (0, 0), (rim_width, rim_width), (0, 0)))
        part_real, part_imag = apply_taps(
            padded_bins[0], padded_bins[1], range_taps, spectrum.shape[2]
        )
        refined.append(jnp.stack([part_real, part_imag]))
    turned = refined
    steer_real, steer_imag = steering(beam_index, channel_phase)
    interval = 0
    inv_real, inv_imag = loaded_inverse(turned[interval][0], turned[interval][1], loading)
    weight_real, weight_imag = beam_weights(inv_real, inv_imag, steer_real, steer_imag)
    beam_power = form_beams(
        turned[interval + 1][0], turned[interval + 1][1], weight_real, weight_imag
    )
    partials = [jnp.sum(beam_power, axis=(0, 1))]
    totals = lax.psum(jnp.stack(partials), ("section", "sub"))
    noise_level = totals / (PULSES * turned[0].shape[2])
    return jnp.stack([beam_power / (noise_level[0] + epsilon)])


MESH = pl.DeviceIdType.MESH
bf16 = jnp.bfloat16
f32 = jnp.float32


def fourier_rows(parts):
    index = np.arange(PULSES)
    angle = 2.0 * np.pi / PULSES * (index[:, None] * index[None, :] % PULSES)
    cosine, sine = np.cos(angle), np.sin(angle)
    real_rows = np.concatenate([cosine, sine], axis=1)
    imag_rows = np.concatenate([-sine, cosine], axis=1)
    own = PULSES // parts
    rows = np.stack([real_rows.reshape(parts, own, -1), imag_rows.reshape(parts, own, -1)], axis=1)
    return rows.reshape(2 * PULSES, 2 * PULSES).astype(np.float32)


def split(value):
    high = value.astype(bf16)
    return high, (value - high.astype(f32)).astype(bf16)


def dot3(left_high, left_low, right_high, right_low):
    out = jnp.dot(left_high, right_high, preferred_element_type=f32)
    out = out + jnp.dot(left_high, right_low, preferred_element_type=f32)
    return out + jnp.dot(left_low, right_high, preferred_element_type=f32)


def exact(left, right, dims):
    return lax.dot_general(left, right, (dims, ((), ())), precision=precise, preferred_element_type=f32)


def turned_pair(stacked):
    half = stacked.shape[0] // 2
    return jnp.concatenate([-stacked[half:], stacked[:half]], axis=0)


def kernel(
    sections, subs, gates, channels, bins,
    x_ref, rows_ref, taper_ref, steer_r_ref, steer_i_ref, taps_ref, loading_ref,
    power_ref, total_ref,
    table_h, table_l, steer_h, steer_l, send, recv, filt, beams, inner, scale, sums, gathered,
    send_sem, recv_sem, own_sem, sum_send_sem, sum_recv_sem,
):
    parts = sections * subs
    local_gates = gates // sections
    local_channels = channels // subs
    train = x_ref.shape[0] // 2
    taps = taps_ref.shape[1]
    half = taps // 2
    section = lax.axis_index("section")
    sub = lax.axis_index("sub")
    me = section * subs + sub
    rows = 2 * bins

    def place(step):
        peer = lax.rem(me + step, parts)
        return peer, {"section": peer // subs, "sub": lax.rem(peer, subs)}

    barrier = pltpu.get_barrier_semaphore()
    for step in range(1, parts):
        pl.semaphore_signal(barrier, inc=1, device_id=place(step)[1], device_id_type=MESH)

    high, low = split(rows_ref[...] * taper_ref[...])
    table_h[...] = high
    table_l[...] = low

    def piece(interval, step):
        peer, where = place(step)
        return pltpu.make_async_remote_copy(
            src_ref=send.at[interval, pl.ds(pl.multiple_of(peer * rows, rows), rows)],
            dst_ref=recv.at[interval, me + subs],
            send_sem=send_sem.at[interval, step - 1],
            recv_sem=recv_sem.at[interval, step - 1],
            device_id=where,
            device_id_type=MESH,
        )

    def own_piece(interval):
        return pltpu.make_async_copy(
            send.at[interval, pl.ds(pl.multiple_of(me * rows, rows), rows)],
            recv.at[interval, me + subs],
            own_sem.at[interval],
        )

    for interval in range(INTERVALS):
        start = interval * HOP
        segment = jnp.concatenate(
            [x_ref[start : start + PULSES], x_ref[train + start : train + start + PULSES]], axis=0
        )
        high, low = split(segment)
        send[interval] = dot3(table_h[...], table_l[...], high, low)
        if interval == 0:
            pl.semaphore_wait(barrier, parts - 1)
        own_piece(interval).start()
        for step in range(1, parts):
            piece(interval, step).start()

    for interval in range(INTERVALS):
        for slot in range(subs):
            recv[interval, slot] = jnp.zeros(recv.shape[2:], f32)
            recv[interval, subs + parts + slot] = jnp.zeros(recv.shape[2:], f32)

    steer_r, steer_i = steer_r_ref[...], steer_i_ref[...]
    steer_both = jnp.concatenate(
        [
            jnp.concatenate([steer_r, steer_i], axis=1),
            jnp.concatenate([-steer_i, steer_r], axis=1),
        ],
        axis=0,
    )
    high, low = split(steer_both)
    steer_h[...] = high
    steer_l[...] = low

    def refine(interval, sign):
        own_piece(interval).wait()
        for step in range(1, parts):
            piece(interval, step).wait()

        def one(slot, carry):
            here = slot // subs
            columns = lax.rem(slot, subs)

            def gate(offset):
                shift = offset // local_gates
                column = (offset % local_gates) * local_channels
                block = recv[interval, slot + subs * (1 + shift), :, column : column + local_channels]
                return block[:bins], block[bins:]

            around = {offset: gate(offset) for offset in range(-half, local_gates + half)}
            for local in range(local_gates):
                real = jnp.zeros((bins, local_channels), f32)
                imag = jnp.zeros((bins, local_channels), f32)
                for tap in range(taps):
                    part_r, part_i = around[local + tap - half]
                    tap_r, tap_i = taps_ref[0, tap], taps_ref[1, tap]
                    real = real + tap_r * part_r - tap_i * part_i
                    imag = imag + tap_r * part_i + tap_i * part_r
                row = pl.multiple_of((here * local_gates + local) * bins, bins)
                filt[interval, columns, pl.ds(row, bins)] = real
                filt[interval, columns, pl.ds(row + gates * bins, bins)] = sign * imag
            return carry

        lax.fori_loop(0, parts, one, 0)
        count = gates * bins
        both = jnp.concatenate(
            [filt[interval, block, start : start + count] for start in (0, count) for block in range(subs)],
            axis=1,
        )
        high, low = split(both)
        out = dot3(high, low, steer_h[...], steer_l[...])
        lanes = beams.shape[2]
        blocks = beams.shape[0]
        for block in range(2 * blocks):
            start = block // blocks * count
            beams[block % blocks, start : start + count] = out[:, block * lanes : (block + 1) * lanes]

    def rows_of(ref, index):
        return jnp.concatenate(
            [ref[block, pl.ds(index, 2 * gates, stride=bins), :] for block in range(ref.shape[0])], axis=1
        )

    def solve(index, carry):
        data = rows_of(filt.at[0], index)
        aside = turned_pair(data)
        trace = jnp.sum(jnp.sum(data * data, axis=0, keepdims=True), axis=1, keepdims=True) / gates
        loaded = loading_ref[0] * trace / channels
        data_h, data_l = split(data)
        aside_h, aside_l = split(aside)
        left = jnp.concatenate([data_h, data_l, data_h, data_l], axis=0)
        right_r = jnp.concatenate([data_h, data_h, data_l, data_l], axis=0)
        right_i = jnp.concatenate([aside_h, aside_h, aside_l, aside_l], axis=0)
        dims = (((0,), (0,)), ((), ()))
        cov_r = lax.dot_general(left, right_r, dims, preferred_element_type=f32)
        cov_i = lax.dot_general(left, right_i, dims, preferred_element_type=f32)
        sums_of = jnp.sum(jnp.abs(cov_r) + jnp.abs(cov_i), axis=0, keepdims=True)
        bound = jnp.max(sums_of, axis=1, keepdims=True) / gates + loaded
        unit = 1.0 / (gates * bound)
        shift = loaded / bound
        across = ((1,), (1,))
        gram = (exact(data, data, across) + exact(aside, aside, across)) * unit
        square = exact(gram, gram, ((1,), (0,)))
        row_index = lax.broadcasted_iota(jnp.int32, gram.shape, 0)
        column_index = lax.broadcasted_iota(jnp.int32, gram.shape, 1)
        zeroth = jnp.where(row_index == column_index, -6.0 + 8.0 * shift - 3.0 * shift * shift, 0.0)
        poly = zeroth + (4.0 - 3.0 * shift) * gram - square
        plain = 4.0 - 6.0 * shift + 4.0 * shift * shift - shift * shift * shift
        toward = rows_of(beams, index)
        moved = exact(poly, toward, ((1,), (0,)))
        gain = plain * channels + unit * jnp.sum(toward * moved, axis=0, keepdims=True)
        inner[index] = moved * (unit / gain)
        scale[index] = plain / gain
        return carry

    def form(index, carry):
        data = rows_of(filt.at[0], index)
        later = rows_of(filt.at[1], index)
        across = ((1,), (1,))
        cross = exact(later, data, across) + exact(turned_pair(later), turned_pair(data), across)
        out = rows_of(beams, index) * scale[index] + exact(cross, inner[index], ((1,), (0,)))
        power = out[:gates] * out[:gates] + out[gates:] * out[gates:]
        power_ref[index] = power
        return carry + jnp.sum(power.reshape(gates // 8, 8, -1), axis=0)

    refine(0, 1.0)
    lax.fori_loop(0, bins, solve, 0)
    refine(1, -1.0)
    sums[...] = lax.fori_loop(0, bins, form, jnp.zeros(sums.shape, f32))

    def sum_piece(step):
        return pltpu.make_async_remote_copy(
            src_ref=sums,
            dst_ref=gathered.at[step - 1],
            send_sem=sum_send_sem.at[step - 1],
            recv_sem=sum_recv_sem.at[step - 1],
            device_id=place(step)[1],
            device_id_type=MESH,
        )

    for step in range(1, parts):
        sum_piece(step).start()
    total = sums[...]
    for step in range(1, parts):
        sum_piece(step).wait()
    for step in range(1, parts):
        total = total + gathered[step - 1]
    total_ref[...] = total


def fused(sections, subs, echoes, range_taps, pulse_taper, channel_phase, loading, beam_index):
    parts = sections * subs
    local_gates, local_channels = echoes.shape[2:]
    gates, channels = local_gates * sections, local_channels * subs
    bins = PULSES // parts
    beam_count = beam_index.shape[0]
    flat = echoes.reshape(2 * echoes.shape[1], local_gates * local_channels)
    steer_real, steer_imag = steering(beam_index, channel_phase)
    taper = jnp.concatenate([pulse_taper, pulse_taper])[None, :]
    vmem = pl.BlockSpec(memory_space=pltpu.VMEM)
    smem = pl.BlockSpec(memory_space=pltpu.SMEM)
    power, total = pl.pallas_call(
        functools.partial(kernel, sections, subs, gates, channels, bins),
        out_shape=(
            jax.ShapeDtypeStruct((bins, gates, beam_count), f32),
            jax.ShapeDtypeStruct((8, beam_count), f32),
        ),
        in_specs=[vmem] * 5 + [smem] * 2,
        out_specs=(vmem, vmem),
        scratch_shapes=[
            pltpu.VMEM((2 * PULSES, 2 * PULSES), bf16),
            pltpu.VMEM((2 * PULSES, 2 * PULSES), bf16),
            pltpu.VMEM((2 * channels, 2 * beam_count), bf16),
            pltpu.VMEM((2 * channels, 2 * beam_count), bf16),
            pltpu.VMEM((INTERVALS, 2 * PULSES, local_gates * local_channels), f32),
            pltpu.VMEM((INTERVALS, parts + 2 * subs, 2 * bins, local_gates * local_channels), f32),
            pltpu.VMEM((INTERVALS, subs, 2 * gates * bins, local_channels), f32),
            pltpu.VMEM((beam_count // 128, 2 * gates * bins, 128), f32),
            pltpu.VMEM((bins, 2 * gates, beam_count), f32),
            pltpu.VMEM((bins, 1, beam_count), f32),
            pltpu.VMEM((8, beam_count), f32),
            pltpu.VMEM((parts - 1, 8, beam_count), f32),
            pltpu.SemaphoreType.DMA((INTERVALS, parts - 1)),
            pltpu.SemaphoreType.DMA((INTERVALS, parts - 1)),
            pltpu.SemaphoreType.DMA((INTERVALS,)),
            pltpu.SemaphoreType.DMA((parts - 1,)),
            pltpu.SemaphoreType.DMA((parts - 1,)),
        ],
        compiler_params=pltpu.CompilerParams(
            collective_id=0, has_side_effects=True, vmem_limit_bytes=56 * 2**20
        ),
        name="beams",
    )(flat, jnp.asarray(fourier_rows(parts)), taper, steer_real, steer_imag, range_taps, loading)
    noise_level = jnp.sum(total, axis=0) / (PULSES * gates)
    return (power / (noise_level + epsilon))[None]


def solution(mesh):
    sections, subs = mesh.shape["section"], mesh.shape["sub"]
    parts = sections * subs

    def body(echoes, *rest):
        local_gates, local_channels = echoes.shape[2:]
        gates, channels = local_gates * sections, local_channels * subs
        fits = (
            PULSES % parts == 0
            and (PULSES // parts) % 8 == 0
            and gates % 8 == 0
            and 2 * gates <= channels
            and local_channels == 128
            and rest[-1].shape[0] % 128 == 0
            and local_gates >= rest[0].shape[1] // 2
            and channels == rest[-1].shape[0]
        )
        if fits:
            return fused(sections, subs, echoes, *rest)
        return on_device(echoes, *rest)

    in_specs = (P("groups", None, "section", "sub"), P(), P(), P(), P(), P())
    out_specs = P("groups", ("section", "sub"), None, None)
    return jax.shard_map(
        body, mesh=mesh, in_specs=in_specs, out_specs=out_specs, check_vma=False
    )
```

```python
import functools
import math

import jax
import jax.numpy as jnp
import numpy as np
from jax import lax
from jax.experimental import pallas as pl
from jax.experimental.pallas import tpu as pltpu
from jax.sharding import PartitionSpec as P

PULSES = 256
INTERVALS = 2
ITERS = 2
LOOKS = 1024
HOP = 128


precise = lax.Precision.HIGHEST
epsilon = 1e-06


def apply_taps(pad_real, pad_imag, range_taps, gate_count):
    axis_gates = pad_real.ndim - 2
    shape_out = pad_real.shape[:axis_gates] + (gate_count,) + pad_real.shape[axis_gates + 1 :]
    out_real = jnp.zeros(shape_out, jnp.float32)
    out_imag = jnp.zeros(shape_out, jnp.float32)
    for offset in range(range_taps.shape[1]):
        part_real = lax.slice_in_dim(pad_real, offset, offset + gate_count, axis=axis_gates)
        part_imag = lax.slice_in_dim(pad_imag, offset, offset + gate_count, axis=axis_gates)
        out_real = out_real + range_taps[0, offset] * part_real - range_taps[1, offset] * part_imag
        out_imag = out_imag + range_taps[0, offset] * part_imag + range_taps[1, offset] * part_real
    return (out_real, out_imag)


def doppler_table(pulse_taper):
    pulse_count = pulse_taper.shape[0]
    pulse_index = jnp.arange(pulse_count, dtype=jnp.int32)
    product = pulse_index[:, None] * pulse_index[None, :] % pulse_count
    phase_angle = 2.0 * math.pi / pulse_count * product.astype(jnp.float32)
    cosine = jnp.cos(phase_angle) * pulse_taper[None, :]
    sine_part = jnp.sin(phase_angle) * pulse_taper[None, :]
    upper_rows = jnp.concatenate([cosine, sine_part], axis=1)
    lower_rows = jnp.concatenate([-sine_part, cosine], axis=1)
    return jnp.concatenate([upper_rows, lower_rows], axis=0)


def transform(doppler, segment):
    shape_in = segment.shape
    flattened = segment.reshape(shape_in[0] * shape_in[1], -1)
    result = jnp.dot(doppler, flattened, precision=precise, preferred_element_type=jnp.float32)
    return result.reshape(shape_in)


def batched(first, second):
    return jnp.einsum("dij,djk->dik", first, second, precision=precise)


def complex_product(left_real, left_imag, right_real, right_imag):
    out_real = batched(left_real, right_real) - batched(left_imag, right_imag)
    out_imag = batched(left_real, right_imag) + batched(left_imag, right_real)
    return (out_real, out_imag)


def gram_product(first, second):
    return jnp.einsum("dgi,dgj->dij", first, second, precision=precise)


def loaded_inverse(real_part, imag_part, loading):
    gate_count = real_part.shape[1]
    channels = real_part.shape[2]
    cov_real = (
        gram_product(real_part, real_part) + gram_product(imag_part, imag_part)
    ) / gate_count
    cov_imag = (
        gram_product(real_part, imag_part) - gram_product(imag_part, real_part)
    ) / gate_count
    identity = jnp.eye(channels, dtype=jnp.float32)
    trace_sum = jnp.sum(cov_real * identity[None], axis=(1, 2))
    cov_real = cov_real + (loading[0] * trace_sum / channels)[:, None, None] * identity[None]
    row_bound = jnp.max(jnp.sum(jnp.abs(cov_real) + jnp.abs(cov_imag), axis=2), axis=1)
    inv_real = identity[None] / row_bound[:, None, None]
    inv_imag = jnp.zeros_like(inv_real)
    for newton_step in range(ITERS):
        prod_real, prod_imag = complex_product(cov_real, cov_imag, inv_real, inv_imag)
        inv_real, inv_imag = complex_product(
            inv_real, inv_imag, 2.0 * identity[None] - prod_real, -prod_imag
        )
    return (inv_real, inv_imag)


def steering(beam_index, channel_phase):
    channels = channel_phase.shape[0]
    direction = -1.0 + (2.0 * beam_index.astype(jnp.float32) + 1.0) / LOOKS
    phase_angle = (
        math.pi * jnp.arange(channels, dtype=jnp.float32)[:, None] * direction[None, :]
        + channel_phase[:, None]
    )
    return (jnp.cos(phase_angle), jnp.sin(phase_angle))


def beam_weights(inv_real, inv_imag, steer_real, steer_imag):
    weight_real = jnp.einsum("dij,jb->dib", inv_real, steer_real, precision=precise) - jnp.einsum(
        "dij,jb->dib", inv_imag, steer_imag, precision=precise
    )
    weight_imag = jnp.einsum("dij,jb->dib", inv_real, steer_imag, precision=precise) + jnp.einsum(
        "dij,jb->dib", inv_imag, steer_real, precision=precise
    )
    gain_norm = jnp.sum(steer_real[None] * weight_real + steer_imag[None] * weight_imag, axis=1)
    return (weight_real / gain_norm[:, None, :], weight_imag / gain_norm[:, None, :])


def form_beams(data_real, data_imag, weight_real, weight_imag):
    out_real = jnp.einsum("dgc,dcb->dgb", data_real, weight_real, precision=precise) + jnp.einsum(
        "dgc,dcb->dgb", data_imag, weight_imag, precision=precise
    )
    out_imag = jnp.einsum("dgc,dcb->dgb", data_imag, weight_real, precision=precise) - jnp.einsum(
        "dgc,dcb->dgb", data_real, weight_imag, precision=precise
    )
    return out_real * out_real + out_imag * out_imag


def on_device(echoes, range_taps, pulse_taper, channel_phase, loading, beam_index):
    rim_width = range_taps.shape[1] // 2
    doppler = doppler_table(pulse_taper)
    spectra = [
        transform(
            doppler, lax.slice_in_dim(echoes, interval * HOP, interval * HOP + PULSES, axis=1)
        )
        for interval in range(INTERVALS)
    ]
    turned = [
        lax.all_to_all(
            lax.all_to_all(spectrum, "section", split_axis=1, concat_axis=2, tiled=True),
            "sub",
            split_axis=1,
            concat_axis=3,
            tiled=True,
        )
        for spectrum in spectra
    ]
    refined = []
    for spectrum in turned:
        padded_bins = jnp.pad(spectrum, ((0, 0), (0, 0), (rim_width, rim_width), (0, 0)))
        part_real, part_imag = apply_taps(
            padded_bins[0], padded_bins[1], range_taps, spectrum.shape[2]
        )
        refined.append(jnp.stack([part_real, part_imag]))
    turned = refined
    steer_real, steer_imag = steering(beam_index, channel_phase)
    interval = 0
    inv_real, inv_imag = loaded_inverse(turned[interval][0], turned[interval][1], loading)
    weight_real, weight_imag = beam_weights(inv_real, inv_imag, steer_real, steer_imag)
    beam_power = form_beams(
        turned[interval + 1][0], turned[interval + 1][1], weight_real, weight_imag
    )
    partials = [jnp.sum(beam_power, axis=(0, 1))]
    totals = lax.psum(jnp.stack(partials), ("section", "sub"))
    noise_level = totals / (PULSES * turned[0].shape[2])
    return jnp.stack([beam_power / (noise_level[0] + epsilon)])


MESH = pl.DeviceIdType.MESH
bf16 = jnp.bfloat16
f32 = jnp.float32
BLOCK = 8


def fourier_rows(parts):
    index = np.arange(PULSES)
    angle = 2.0 * np.pi / PULSES * (index[:, None] * index[None, :] % PULSES)
    cosine, sine = np.cos(angle), np.sin(angle)
    real_rows = np.concatenate([cosine, sine], axis=1)
    imag_rows = np.concatenate([-sine, cosine], axis=1)
    split_rows = [part.reshape(parts, -1, BLOCK, 2 * PULSES) for part in (real_rows, imag_rows)]
    rows = np.stack(split_rows, axis=2).transpose(1, 0, 2, 3, 4)
    return rows.reshape(2 * PULSES, 2 * PULSES).astype(np.float32)


def split(value):
    high = value.astype(bf16)
    return high, (value - high.astype(f32)).astype(bf16)


def dot3(left_high, left_low, right_high, right_low):
    out = jnp.dot(left_high, right_high, preferred_element_type=f32)
    out = out + jnp.dot(left_high, right_low, preferred_element_type=f32)
    return out + jnp.dot(left_low, right_high, preferred_element_type=f32)


def dot3_across(left_high, left_low, right_high, right_low):
    dims = (((1,), (1,)), ((), ()))
    out = lax.dot_general(left_high, right_high, dims, preferred_element_type=f32)
    out = out + lax.dot_general(left_high, right_low, dims, preferred_element_type=f32)
    return out + lax.dot_general(left_low, right_high, dims, preferred_element_type=f32)


def exact(left, right, dims):
    return lax.dot_general(left, right, (dims, ((), ())), precision=precise, preferred_element_type=f32)


def turned_pair(stacked):
    half = stacked.shape[0] // 2
    return jnp.concatenate([-stacked[half:], stacked[:half]], axis=0)


def kernel(
    sections, subs, gates, channels, bins,
    x_hbm, rows_hbm, taper_ref, phase_ref, beam_ref, taps_ref, loading_ref,
    power_hbm, noise_ref,
    x_ref, rows_ref, table_h, table_l, steer_h, steer_l, send, recv, filt, beams,
    conj_h, conj_l, inner_h, inner_l, scale, power_ref, sums, gathered,
    x_sem, rows_sem, send_sem, recv_sem, own_sem, sum_send_sem, sum_recv_sem, out_sem,
):
    parts = sections * subs
    local_gates = gates // sections
    local_channels = channels // subs
    train = x_ref.shape[0] // (2 * local_gates)
    taps = taps_ref.shape[1]
    half = taps // 2
    groups_of_bins = bins // BLOCK
    section = lax.axis_index("section")
    sub = lax.axis_index("sub")
    me = section * subs + sub
    rows = 2 * BLOCK
    steps = list(range(parts - 1, 0, -1))

    def place(step):
        peer = me ^ step
        return peer, {"section": peer // subs, "sub": lax.rem(peer, subs)}

    first = PULSES * local_gates
    rest = (train - PULSES) * local_gates
    x_copies = []
    for number, (start, length) in enumerate(
        [(0, first), (train * local_gates, first), (first, rest), (train * local_gates + first, rest)]
    ):
        x_copies.append(
            pltpu.make_async_copy(
                x_hbm.at[pl.ds(start, length)], x_ref.at[pl.ds(start, length)], x_sem.at[number]
            )
        )
    rows_copy = pltpu.make_async_copy(rows_hbm, rows_ref, rows_sem)
    rows_copy.start()
    for copy in x_copies:
        copy.start()
    barrier = pltpu.get_barrier_semaphore()
    for step in steps:
        pl.semaphore_signal(barrier, inc=1, device_id=place(step)[1], device_id_type=MESH)

    taper = jnp.concatenate([taper_ref[...], taper_ref[...]], axis=1)
    rows_copy.wait()
    high, low = split(rows_ref[...] * taper)
    table_h[...] = high
    table_l[...] = low

    def piece(unit, step):
        peer, where = place(step)
        return pltpu.make_async_remote_copy(
            src_ref=send.at[unit, pl.ds(pl.multiple_of(peer * rows, rows), rows)],
            dst_ref=recv.at[unit, me + subs],
            send_sem=send_sem.at[unit, step - 1],
            recv_sem=recv_sem.at[unit, step - 1],
            device_id=where,
            device_id_type=MESH,
        )

    def own_piece(unit):
        return pltpu.make_async_copy(
            send.at[unit, pl.ds(pl.multiple_of(me * rows, rows), rows)],
            recv.at[unit, me + subs],
            own_sem.at[unit],
        )

    for interval in range(INTERVALS):
        x_copies[2 * interval].wait()
        x_copies[2 * interval + 1].wait()
        segment = jnp.concatenate(
            [
                jnp.concatenate(
                    [
                        x_ref[
                            pl.ds((part * train + interval * HOP) * local_gates + gate, PULSES, stride=local_gates), :
                        ]
                        for gate in range(local_gates)
                    ],
                    axis=1,
                )
                for part in range(2)
            ],
            axis=0,
        )
        high, low = split(segment)
        for group in range(groups_of_bins):
            unit = interval * groups_of_bins + group
            of_group = slice(group * parts * rows, (group + 1) * parts * rows)
            send[unit] = dot3(table_h[of_group], table_l[of_group], high, low)
            if unit == 0:
                pl.semaphore_wait(barrier, parts - 1)
            for step in steps:
                piece(unit, step).start()
            own_piece(unit).start()

    for unit in range(recv.shape[0]):
        for slot in range(subs):
            recv[unit, slot] = jnp.zeros(recv.shape[2:], f32)
            recv[unit, subs + parts + slot] = jnp.zeros(recv.shape[2:], f32)

    direction = -1.0 + (2.0 * beam_ref[...].astype(f32) + 1.0) / LOOKS
    beam_count = direction.shape[1]
    channel = lax.broadcasted_iota(jnp.int32, (channels, beam_count), 0).astype(f32)
    phase = jnp.transpose(jnp.broadcast_to(phase_ref[...], (beam_count, channels)))
    angle = math.pi * channel * direction + phase
    steer_r, steer_i = jnp.cos(angle), jnp.sin(angle)
    steer_both = jnp.concatenate(
        [
            jnp.concatenate([steer_r, steer_i], axis=1),
            jnp.concatenate([-steer_i, steer_r], axis=1),
        ],
        axis=0,
    )
    high, low = split(steer_both)
    steer_h[...] = high
    steer_l[...] = low

    def refine(unit, sign):
        own_piece(unit).wait()
        for step in steps:
            piece(unit, step).wait()

        def one(slot, carry):
            here = slot // subs
            columns = lax.rem(slot, subs)

            def gate(offset):
                shift = offset // local_gates
                column = (offset % local_gates) * local_channels
                block = recv[unit, slot + subs * (1 + shift), :, column : column + local_channels]
                return block[:BLOCK], block[BLOCK:]

            around = {offset: gate(offset) for offset in range(-half, local_gates + half)}
            for local in range(local_gates):
                real = jnp.zeros((BLOCK, local_channels), f32)
                imag = jnp.zeros((BLOCK, local_channels), f32)
                for tap in range(taps):
                    part_r, part_i = around[local + tap - half]
                    tap_r, tap_i = taps_ref[0, tap], taps_ref[1, tap]
                    real = real + tap_r * part_r - tap_i * part_i
                    imag = imag + tap_r * part_i + tap_i * part_r
                row = pl.multiple_of((here * local_gates + local) * BLOCK, BLOCK)
                filt[columns, pl.ds(row, BLOCK)] = real
                filt[columns, pl.ds(row + gates * BLOCK, BLOCK)] = sign * imag
            return carry

        lax.fori_loop(0, parts, one, 0, unroll=2)
        count = gates * BLOCK
        both = jnp.concatenate(
            [filt[block, start : start + count] for start in (0, count) for block in range(subs)],
            axis=1,
        )
        high, low = split(both)
        out = dot3(high, low, steer_h[...], steer_l[...])
        lanes = beams.shape[2]
        blocks = beams.shape[0]
        for block in range(2 * blocks):
            start = block // blocks * count
            beams[block % blocks, start : start + count] = out[:, block * lanes : (block + 1) * lanes]

    def rows_of(ref, index):
        return jnp.concatenate(
            [ref[block, pl.ds(index, 2 * gates, stride=BLOCK), :] for block in range(ref.shape[0])], axis=1
        )

    def solve(group, index, carry):
        data = rows_of(filt, index)
        aside = turned_pair(data)
        trace = jnp.sum(jnp.sum(data * data, axis=0, keepdims=True), axis=1, keepdims=True) / gates
        loaded = loading_ref[0] * trace / channels
        data_h, data_l = split(data)
        aside_h, aside_l = split(aside)
        left = jnp.concatenate([data_h, data_l, data_h, data_l], axis=0)
        right_r = jnp.concatenate([data_h, data_h, data_l, data_l], axis=0)
        right_i = jnp.concatenate([aside_h, aside_h, aside_l, aside_l], axis=0)
        dims = (((0,), (0,)), ((), ()))
        cov_r = lax.dot_general(left, right_r, dims, preferred_element_type=f32)
        cov_i = lax.dot_general(left, right_i, dims, preferred_element_type=f32)
        sums_of = jnp.sum(jnp.abs(cov_r) + jnp.abs(cov_i), axis=0, keepdims=True)
        bound = jnp.max(sums_of, axis=1, keepdims=True) / gates + loaded
        unit = 1.0 / (gates * bound)
        shift = loaded / bound
        full_h = jnp.concatenate([data_h, aside_h], axis=1)
        full_l = jnp.concatenate([data_l, aside_l], axis=1)
        gram = dot3_across(full_h, full_l, full_h, full_l) * unit
        square = exact(gram, gram, ((1,), (0,)))
        row_index = lax.broadcasted_iota(jnp.int32, gram.shape, 0)
        column_index = lax.broadcasted_iota(jnp.int32, gram.shape, 1)
        zeroth = jnp.where(row_index == column_index, -6.0 + 8.0 * shift - 3.0 * shift * shift, 0.0)
        poly = zeroth + (4.0 - 3.0 * shift) * gram - square
        plain = 4.0 - 6.0 * shift + 4.0 * shift * shift - shift * shift * shift
        toward = rows_of(beams, index)
        moved = exact(poly, toward, ((1,), (0,)))
        gain = plain * channels + unit * jnp.sum(toward * moved, axis=0, keepdims=True)
        place_of = group * BLOCK + index
        high, low = split(moved * (unit / gain))
        inner_h[place_of] = high
        inner_l[place_of] = low
        conj_h[place_of] = full_h
        conj_l[place_of] = full_l
        scale[place_of] = plain / gain
        return carry

    def form(group, index, carry):
        place_of = group * BLOCK + index
        later = rows_of(filt, index)
        high, low = split(jnp.concatenate([later, turned_pair(later)], axis=1))
        cross = dot3_across(high, low, conj_h[place_of], conj_l[place_of])
        high, low = split(cross)
        out = rows_of(beams, index) * scale[place_of] + dot3(high, low, inner_h[place_of], inner_l[place_of])
        power = out[:gates] * out[:gates] + out[gates:] * out[gates:]
        power_ref[place_of] = power
        return carry + jnp.sum(power.reshape(gates // 8, 8, -1), axis=0)

    for group in range(groups_of_bins):
        refine(group, 1.0)
        lax.fori_loop(0, BLOCK, functools.partial(solve, group), 0, unroll=2)
    total = jnp.zeros(sums.shape, f32)
    out_copies = []
    for group in range(groups_of_bins):
        refine(groups_of_bins + group, -1.0)
        total = lax.fori_loop(0, BLOCK, functools.partial(form, group), total, unroll=4)
        span = pl.ds(group * BLOCK, BLOCK)
        out_copies.append(pltpu.make_async_copy(power_ref.at[span], power_hbm.at[span], out_sem.at[group]))
        if group < groups_of_bins - 1:
            out_copies[-1].start()
    sums[...] = total

    def sum_piece(step):
        return pltpu.make_async_remote_copy(
            src_ref=sums,
            dst_ref=gathered.at[step - 1],
            send_sem=sum_send_sem.at[step - 1],
            recv_sem=sum_recv_sem.at[step - 1],
            device_id=place(step)[1],
            device_id_type=MESH,
        )

    for step in steps:
        sum_piece(step).start()
    out_copies[-1].start()
    for step in steps:
        sum_piece(step).wait()
    for step in steps:
        total = total + gathered[step - 1]
    noise_ref[...] = jnp.sum(total, axis=0, keepdims=True) / (PULSES * gates) + epsilon
    for copy in out_copies:
        copy.wait()


def fused(sections, subs, echoes, range_taps, pulse_taper, channel_phase, loading, beam_index):
    parts = sections * subs
    local_gates, local_channels = echoes.shape[2:]
    gates, channels = local_gates * sections, local_channels * subs
    bins = PULSES // parts
    beam_count = beam_index.shape[0]
    units = INTERVALS * bins // BLOCK
    width = local_gates * local_channels
    flat = echoes.reshape(2 * echoes.shape[1] * local_gates, local_channels)
    vmem = pl.BlockSpec(memory_space=pltpu.VMEM)
    smem = pl.BlockSpec(memory_space=pltpu.SMEM)
    whole = pl.BlockSpec(memory_space=pl.ANY)
    power, noise_level = pl.pallas_call(
        functools.partial(kernel, sections, subs, gates, channels, bins),
        out_shape=(
            jax.ShapeDtypeStruct((bins, gates, beam_count), f32),
            jax.ShapeDtypeStruct((1, beam_count), f32),
        ),
        in_specs=[whole] * 2 + [vmem] * 3 + [smem] * 2,
        out_specs=(whole, vmem),
        scratch_shapes=[
            pltpu.VMEM(flat.shape, f32),
            pltpu.VMEM((2 * PULSES, 2 * PULSES), f32),
            pltpu.VMEM((2 * PULSES, 2 * PULSES), bf16),
            pltpu.VMEM((2 * PULSES, 2 * PULSES), bf16),
            pltpu.VMEM((2 * channels, 2 * beam_count), bf16),
            pltpu.VMEM((2 * channels, 2 * beam_count), bf16),
            pltpu.VMEM((units, parts * 2 * BLOCK, width), f32),
            pltpu.VMEM((units, parts + 2 * subs, 2 * BLOCK, width), f32),
            pltpu.VMEM((subs, 2 * gates * BLOCK, local_channels), f32),
            pltpu.VMEM((beam_count // 128, 2 * gates * BLOCK, 128), f32),
            pltpu.VMEM((bins, 2 * gates, 2 * channels), bf16),
            pltpu.VMEM((bins, 2 * gates, 2 * channels), bf16),
            pltpu.VMEM((bins, 2 * gates, beam_count), bf16),
            pltpu.VMEM((bins, 2 * gates, beam_count), bf16),
            pltpu.VMEM((bins, 1, beam_count), f32),
            pltpu.VMEM((bins, gates, beam_count), f32),
            pltpu.VMEM((8, beam_count), f32),
            pltpu.VMEM((parts - 1, 8, beam_count), f32),
            pltpu.SemaphoreType.DMA((4,)),
            pltpu.SemaphoreType.DMA,
            pltpu.SemaphoreType.DMA((units, parts - 1)),
            pltpu.SemaphoreType.DMA((units, parts - 1)),
            pltpu.SemaphoreType.DMA((units,)),
            pltpu.SemaphoreType.DMA((parts - 1,)),
            pltpu.SemaphoreType.DMA((parts - 1,)),
            pltpu.SemaphoreType.DMA((bins // BLOCK,)),
        ],
        compiler_params=pltpu.CompilerParams(
            collective_id=0, has_side_effects=True, vmem_limit_bytes=56 * 2**20
        ),
        name="beams",
    )(
        flat, jnp.asarray(fourier_rows(parts)), pulse_taper[None, :], channel_phase[None, :], beam_index[None, :],
        range_taps, loading,
    )
    return (power / noise_level)[None]


def solution(mesh):
    sections, subs = mesh.shape["section"], mesh.shape["sub"]
    parts = sections * subs

    def body(echoes, *rest):
        local_gates, local_channels = echoes.shape[2:]
        gates, channels = local_gates * sections, local_channels * subs
        fits = (
            parts & (parts - 1) == 0
            and PULSES % parts == 0
            and (PULSES // parts) % BLOCK == 0
            and echoes.shape[1] == (INTERVALS - 1) * HOP + PULSES
            and INTERVALS == 2
            and ITERS == 2
            and gates % 8 == 0
            and 2 * gates <= channels
            and local_channels == 128
            and rest[-1].shape[0] % 128 == 0
            and local_gates >= rest[0].shape[1] // 2
            and channels == rest[-1].shape[0]
        )
        if fits:
            return fused(sections, subs, echoes, *rest)
        return on_device(echoes, *rest)

    in_specs = (P("groups", None, "section", "sub"), P(), P(), P(), P(), P())
    out_specs = P("groups", ("section", "sub"), None, None)
    return jax.shard_map(
        body, mesh=mesh, in_specs=in_specs, out_specs=out_specs, check_vma=False
    )
```

```python
import functools
import math

import jax
import jax.numpy as jnp
import numpy as np
from jax import lax
from jax.experimental import pallas as pl
from jax.experimental.pallas import tpu as pltpu
from jax.sharding import PartitionSpec as P

PULSES = 256
INTERVALS = 2
ITERS = 2
LOOKS = 1024
HOP = 128


precise = lax.Precision.HIGHEST
epsilon = 1e-06


def apply_taps(pad_real, pad_imag, range_taps, gate_count):
    axis_gates = pad_real.ndim - 2
    shape_out = pad_real.shape[:axis_gates] + (gate_count,) + pad_real.shape[axis_gates + 1 :]
    out_real = jnp.zeros(shape_out, jnp.float32)
    out_imag = jnp.zeros(shape_out, jnp.float32)
    for offset in range(range_taps.shape[1]):
        part_real = lax.slice_in_dim(pad_real, offset, offset + gate_count, axis=axis_gates)
        part_imag = lax.slice_in_dim(pad_imag, offset, offset + gate_count, axis=axis_gates)
        out_real = out_real + range_taps[0, offset] * part_real - range_taps[1, offset] * part_imag
        out_imag = out_imag + range_taps[0, offset] * part_imag + range_taps[1, offset] * part_real
    return (out_real, out_imag)


def doppler_table(pulse_taper):
    pulse_count = pulse_taper.shape[0]
    pulse_index = jnp.arange(pulse_count, dtype=jnp.int32)
    product = pulse_index[:, None] * pulse_index[None, :] % pulse_count
    phase_angle = 2.0 * math.pi / pulse_count * product.astype(jnp.float32)
    cosine = jnp.cos(phase_angle) * pulse_taper[None, :]
    sine_part = jnp.sin(phase_angle) * pulse_taper[None, :]
    upper_rows = jnp.concatenate([cosine, sine_part], axis=1)
    lower_rows = jnp.concatenate([-sine_part, cosine], axis=1)
    return jnp.concatenate([upper_rows, lower_rows], axis=0)


def transform(doppler, segment):
    shape_in = segment.shape
    flattened = segment.reshape(shape_in[0] * shape_in[1], -1)
    result = jnp.dot(doppler, flattened, precision=precise, preferred_element_type=jnp.float32)
    return result.reshape(shape_in)


def batched(first, second):
    return jnp.einsum("dij,djk->dik", first, second, precision=precise)


def complex_product(left_real, left_imag, right_real, right_imag):
    out_real = batched(left_real, right_real) - batched(left_imag, right_imag)
    out_imag = batched(left_real, right_imag) + batched(left_imag, right_real)
    return (out_real, out_imag)


def gram_product(first, second):
    return jnp.einsum("dgi,dgj->dij", first, second, precision=precise)


def loaded_inverse(real_part, imag_part, loading):
    gate_count = real_part.shape[1]
    channels = real_part.shape[2]
    cov_real = (
        gram_product(real_part, real_part) + gram_product(imag_part, imag_part)
    ) / gate_count
    cov_imag = (
        gram_product(real_part, imag_part) - gram_product(imag_part, real_part)
    ) / gate_count
    identity = jnp.eye(channels, dtype=jnp.float32)
    trace_sum = jnp.sum(cov_real * identity[None], axis=(1, 2))
    cov_real = cov_real + (loading[0] * trace_sum / channels)[:, None, None] * identity[None]
    row_bound = jnp.max(jnp.sum(jnp.abs(cov_real) + jnp.abs(cov_imag), axis=2), axis=1)
    inv_real = identity[None] / row_bound[:, None, None]
    inv_imag = jnp.zeros_like(inv_real)
    for newton_step in range(ITERS):
        prod_real, prod_imag = complex_product(cov_real, cov_imag, inv_real, inv_imag)
        inv_real, inv_imag = complex_product(
            inv_real, inv_imag, 2.0 * identity[None] - prod_real, -prod_imag
        )
    return (inv_real, inv_imag)


def steering(beam_index, channel_phase):
    channels = channel_phase.shape[0]
    direction = -1.0 + (2.0 * beam_index.astype(jnp.float32) + 1.0) / LOOKS
    phase_angle = (
        math.pi * jnp.arange(channels, dtype=jnp.float32)[:, None] * direction[None, :]
        + channel_phase[:, None]
    )
    return (jnp.cos(phase_angle), jnp.sin(phase_angle))


def beam_weights(inv_real, inv_imag, steer_real, steer_imag):
    weight_real = jnp.einsum("dij,jb->dib", inv_real, steer_real, precision=precise) - jnp.einsum(
        "dij,jb->dib", inv_imag, steer_imag, precision=precise
    )
    weight_imag = jnp.einsum("dij,jb->dib", inv_real, steer_imag, precision=precise) + jnp.einsum(
        "dij,jb->dib", inv_imag, steer_real, precision=precise
    )
    gain_norm = jnp.sum(steer_real[None] * weight_real + steer_imag[None] * weight_imag, axis=1)
    return (weight_real / gain_norm[:, None, :], weight_imag / gain_norm[:, None, :])


def form_beams(data_real, data_imag, weight_real, weight_imag):
    out_real = jnp.einsum("dgc,dcb->dgb", data_real, weight_real, precision=precise) + jnp.einsum(
        "dgc,dcb->dgb", data_imag, weight_imag, precision=precise
    )
    out_imag = jnp.einsum("dgc,dcb->dgb", data_imag, weight_real, precision=precise) - jnp.einsum(
        "dgc,dcb->dgb", data_real, weight_imag, precision=precise
    )
    return out_real * out_real + out_imag * out_imag


def on_device(echoes, range_taps, pulse_taper, channel_phase, loading, beam_index):
    rim_width = range_taps.shape[1] // 2
    doppler = doppler_table(pulse_taper)
    spectra = [
        transform(
            doppler, lax.slice_in_dim(echoes, interval * HOP, interval * HOP + PULSES, axis=1)
        )
        for interval in range(INTERVALS)
    ]
    turned = [
        lax.all_to_all(
            lax.all_to_all(spectrum, "section", split_axis=1, concat_axis=2, tiled=True),
            "sub",
            split_axis=1,
            concat_axis=3,
            tiled=True,
        )
        for spectrum in spectra
    ]
    refined = []
    for spectrum in turned:
        padded_bins = jnp.pad(spectrum, ((0, 0), (0, 0), (rim_width, rim_width), (0, 0)))
        part_real, part_imag = apply_taps(
            padded_bins[0], padded_bins[1], range_taps, spectrum.shape[2]
        )
        refined.append(jnp.stack([part_real, part_imag]))
    turned = refined
    steer_real, steer_imag = steering(beam_index, channel_phase)
    interval = 0
    inv_real, inv_imag = loaded_inverse(turned[interval][0], turned[interval][1], loading)
    weight_real, weight_imag = beam_weights(inv_real, inv_imag, steer_real, steer_imag)
    beam_power = form_beams(
        turned[interval + 1][0], turned[interval + 1][1], weight_real, weight_imag
    )
    partials = [jnp.sum(beam_power, axis=(0, 1))]
    totals = lax.psum(jnp.stack(partials), ("section", "sub"))
    noise_level = totals / (PULSES * turned[0].shape[2])
    return jnp.stack([beam_power / (noise_level[0] + epsilon)])


MESH = pl.DeviceIdType.MESH
bf16 = jnp.bfloat16
f32 = jnp.float32
BLOCK = 8


def fourier_rows(parts):
    index = np.arange(PULSES)
    angle = 2.0 * np.pi / PULSES * (index[:, None] * index[None, :] % PULSES)
    cosine, sine = np.cos(angle), np.sin(angle)
    real_rows = np.concatenate([cosine, sine], axis=1)
    imag_rows = np.concatenate([-sine, cosine], axis=1)
    split_rows = [part.reshape(parts, -1, BLOCK, 2 * PULSES) for part in (real_rows, imag_rows)]
    rows = np.stack(split_rows, axis=2).transpose(1, 0, 2, 3, 4)
    return rows.reshape(2 * PULSES, 2 * PULSES).astype(np.float32)


def split(value):
    high = value.astype(bf16)
    return high, (value - high.astype(f32)).astype(bf16)


def dot3(left_high, left_low, right_high, right_low):
    out = jnp.dot(left_high, right_high, preferred_element_type=f32)
    out = out + jnp.dot(left_high, right_low, preferred_element_type=f32)
    return out + jnp.dot(left_low, right_high, preferred_element_type=f32)


def dot3_across(left_high, left_low, right_high, right_low):
    dims = (((1,), (1,)), ((), ()))
    out = lax.dot_general(left_high, right_high, dims, preferred_element_type=f32)
    out = out + lax.dot_general(left_high, right_low, dims, preferred_element_type=f32)
    return out + lax.dot_general(left_low, right_high, dims, preferred_element_type=f32)


def exact(left, right, dims):
    return lax.dot_general(left, right, (dims, ((), ())), precision=precise, preferred_element_type=f32)


def turned_pair(stacked):
    half = stacked.shape[0] // 2
    return jnp.concatenate([-stacked[half:], stacked[:half]], axis=0)


def kernel(
    sections, subs, gates, channels, bins,
    x_hbm, rows_hbm, taper_ref, phase_ref, beam_ref, taps_ref, loading_ref,
    power_hbm, noise_ref,
    x_ref, rows_ref, table_h, table_l, steer_h, steer_l, send, recv, filt, beams,
    conj_h, conj_l, inner_h, inner_l, scale, power_ref, sums, gathered,
    x_sem, rows_sem, send_sem, recv_sem, own_sem, sum_send_sem, sum_recv_sem, out_sem,
):
    parts = sections * subs
    local_gates = gates // sections
    local_channels = channels // subs
    train = x_ref.shape[0] // (2 * local_gates)
    taps = taps_ref.shape[1]
    half = taps // 2
    groups_of_bins = bins // BLOCK
    section = lax.axis_index("section")
    sub = lax.axis_index("sub")
    me = section * subs + sub
    rows = 2 * BLOCK
    steps = list(range(parts - 1, 0, -1))

    def place(step):
        peer = me ^ step
        return peer, {"section": peer // subs, "sub": lax.rem(peer, subs)}

    first = PULSES * local_gates
    rest = (train - PULSES) * local_gates
    x_copies = []
    for number, (start, length) in enumerate(
        [(0, first), (train * local_gates, first), (first, rest), (train * local_gates + first, rest)]
    ):
        x_copies.append(
            pltpu.make_async_copy(
                x_hbm.at[pl.ds(start, length)], x_ref.at[pl.ds(start, length)], x_sem.at[number]
            )
        )
    rows_copy = pltpu.make_async_copy(rows_hbm, rows_ref, rows_sem)
    rows_copy.start()
    for copy in x_copies:
        copy.start()
    barrier = pltpu.get_barrier_semaphore()
    for step in steps:
        pl.semaphore_signal(barrier, inc=1, device_id=place(step)[1], device_id_type=MESH)

    taper = jnp.concatenate([taper_ref[...], taper_ref[...]], axis=1)
    rows_copy.wait()
    high, low = split(rows_ref[...] * taper)
    table_h[...] = high
    table_l[...] = low

    def piece(unit, step):
        peer, where = place(step)
        return pltpu.make_async_remote_copy(
            src_ref=send.at[unit, pl.ds(pl.multiple_of(peer * rows, rows), rows)],
            dst_ref=recv.at[unit, me + subs],
            send_sem=send_sem.at[unit, step - 1],
            recv_sem=recv_sem.at[unit, step - 1],
            device_id=where,
            device_id_type=MESH,
        )

    def own_piece(unit):
        return pltpu.make_async_copy(
            send.at[unit, pl.ds(pl.multiple_of(me * rows, rows), rows)],
            recv.at[unit, me + subs],
            own_sem.at[unit],
        )

    for interval in range(INTERVALS):
        x_copies[2 * interval].wait()
        x_copies[2 * interval + 1].wait()
        segment = jnp.concatenate(
            [
                jnp.concatenate(
                    [
                        x_ref[
                            pl.ds((part * train + interval * HOP) * local_gates + gate, PULSES, stride=local_gates), :
                        ]
                        for gate in range(local_gates)
                    ],
                    axis=1,
                )
                for part in range(2)
            ],
            axis=0,
        )
        high, low = split(segment)
        for group in range(groups_of_bins):
            unit = interval * groups_of_bins + group
            of_group = slice(group * parts * rows, (group + 1) * parts * rows)
            send[unit] = dot3(table_h[of_group], table_l[of_group], high, low)
            if unit == 0:
                pl.semaphore_wait(barrier, parts - 1)
            for step in steps:
                piece(unit, step).start()
            own_piece(unit).start()

    for unit in range(recv.shape[0]):
        for slot in range(subs):
            recv[unit, slot] = jnp.zeros(recv.shape[2:], f32)
            recv[unit, subs + parts + slot] = jnp.zeros(recv.shape[2:], f32)

    direction = -1.0 + (2.0 * beam_ref[...].astype(f32) + 1.0) / LOOKS
    beam_count = direction.shape[1]
    channel = lax.broadcasted_iota(jnp.int32, (channels, beam_count), 0).astype(f32)
    phase = jnp.transpose(jnp.broadcast_to(phase_ref[...], (beam_count, channels)))
    angle = math.pi * channel * direction + phase
    steer_r, steer_i = jnp.cos(angle), jnp.sin(angle)
    steer_both = jnp.concatenate(
        [
            jnp.concatenate([steer_r, steer_i], axis=1),
            jnp.concatenate([-steer_i, steer_r], axis=1),
        ],
        axis=0,
    )
    high, low = split(steer_both)
    steer_h[...] = high
    steer_l[...] = low

    def refine(unit, sign):
        own_piece(unit).wait()
        for step in steps:
            piece(unit, step).wait()

        def one(slot, carry):
            here = slot // subs
            columns = lax.rem(slot, subs)

            def gate(offset):
                shift = offset // local_gates
                column = (offset % local_gates) * local_channels
                block = recv[unit, slot + subs * (1 + shift), :, column : column + local_channels]
                return block[:BLOCK], block[BLOCK:]

            around = {offset: gate(offset) for offset in range(-half, local_gates + half)}
            for local in range(local_gates):
                real = jnp.zeros((BLOCK, local_channels), f32)
                imag = jnp.zeros((BLOCK, local_channels), f32)
                for tap in range(taps):
                    part_r, part_i = around[local + tap - half]
                    tap_r, tap_i = taps_ref[0, tap], taps_ref[1, tap]
                    real = real + tap_r * part_r - tap_i * part_i
                    imag = imag + tap_r * part_i + tap_i * part_r
                row = pl.multiple_of((here * local_gates + local) * BLOCK, BLOCK)
                filt[columns, pl.ds(row, BLOCK)] = real
                filt[columns, pl.ds(row + gates * BLOCK, BLOCK)] = sign * imag
            return carry

        lax.fori_loop(0, parts, one, 0, unroll=2)
        count = gates * BLOCK
        both = jnp.concatenate(
            [filt[block, start : start + count] for start in (0, count) for block in range(subs)],
            axis=1,
        )
        high, low = split(both)
        out = dot3(high, low, steer_h[...], steer_l[...])
        lanes = beams.shape[2]
        blocks = beams.shape[0]
        for block in range(2 * blocks):
            start = block // blocks * count
            beams[block % blocks, start : start + count] = out[:, block * lanes : (block + 1) * lanes]

    def rows_of(ref, index):
        return jnp.concatenate(
            [ref[block, pl.ds(index, 2 * gates, stride=BLOCK), :] for block in range(ref.shape[0])], axis=1
        )

    def solve(group, index, carry):
        data = rows_of(filt, index)
        aside = turned_pair(data)
        trace = jnp.sum(jnp.sum(data * data, axis=0, keepdims=True), axis=1, keepdims=True) / gates
        loaded = loading_ref[0] * trace / channels
        data_h, data_l = split(data)
        aside_h, aside_l = split(aside)
        left = jnp.concatenate([data_h, data_l, data_h, data_l], axis=0)
        right_r = jnp.concatenate([data_h, data_h, data_l, data_l], axis=0)
        right_i = jnp.concatenate([aside_h, aside_h, aside_l, aside_l], axis=0)
        dims = (((0,), (0,)), ((), ()))
        cov_r = lax.dot_general(left, right_r, dims, preferred_element_type=f32)
        cov_i = lax.dot_general(left, right_i, dims, preferred_element_type=f32)
        sums_of = jnp.sum(jnp.abs(cov_r) + jnp.abs(cov_i), axis=0, keepdims=True)
        bound = jnp.max(sums_of, axis=1, keepdims=True) / gates + loaded
        unit = 1.0 / (gates * bound)
        shift = loaded / bound
        full_h = jnp.concatenate([data_h, aside_h], axis=1)
        full_l = jnp.concatenate([data_l, aside_l], axis=1)
        gram = dot3_across(full_h, full_l, full_h, full_l) * unit
        square = exact(gram, gram, ((1,), (0,)))
        row_index = lax.broadcasted_iota(jnp.int32, gram.shape, 0)
        column_index = lax.broadcasted_iota(jnp.int32, gram.shape, 1)
        zeroth = jnp.where(row_index == column_index, -6.0 + 8.0 * shift - 3.0 * shift * shift, 0.0)
        poly = zeroth + (4.0 - 3.0 * shift) * gram - square
        plain = 4.0 - 6.0 * shift + 4.0 * shift * shift - shift * shift * shift
        toward = rows_of(beams, index)
        moved = exact(poly, toward, ((1,), (0,)))
        gain = plain * channels + unit * jnp.sum(toward * moved, axis=0, keepdims=True)
        place_of = group * BLOCK + index
        high, low = split(moved * (unit / gain))
        inner_h[place_of] = high
        inner_l[place_of] = low
        conj_h[place_of] = full_h
        conj_l[place_of] = full_l
        scale[place_of] = plain / gain
        return carry

    def form(group, index, carry):
        place_of = group * BLOCK + index
        later = rows_of(filt, index)
        high, low = split(jnp.concatenate([later, turned_pair(later)], axis=1))
        cross = dot3_across(high, low, conj_h[place_of], conj_l[place_of])
        high, low = split(cross)
        out = rows_of(beams, index) * scale[place_of] + dot3(high, low, inner_h[place_of], inner_l[place_of])
        power = out[:gates] * out[:gates] + out[gates:] * out[gates:]
        power_ref[place_of] = power
        return carry + jnp.sum(power.reshape(gates // 8, 8, -1), axis=0)

    for group in range(groups_of_bins):
        refine(group, 1.0)
        lax.fori_loop(0, BLOCK, functools.partial(solve, group), 0, unroll=2)
    total = jnp.zeros((8, sums.shape[1]), f32)
    out_copies = []
    for group in range(groups_of_bins):
        refine(groups_of_bins + group, -1.0)
        total = lax.fori_loop(0, BLOCK, functools.partial(form, group), total, unroll=4)
        span = pl.ds(group * BLOCK, BLOCK)
        out_copies.append(pltpu.make_async_copy(power_ref.at[span], power_hbm.at[span], out_sem.at[group]))
        if group < groups_of_bins - 1:
            out_copies[-1].start()
    total = jnp.sum(total, axis=0, keepdims=True)
    sums[...] = total

    def sum_piece(step):
        return pltpu.make_async_remote_copy(
            src_ref=sums,
            dst_ref=gathered.at[step - 1],
            send_sem=sum_send_sem.at[step - 1],
            recv_sem=sum_recv_sem.at[step - 1],
            device_id=place(step)[1],
            device_id_type=MESH,
        )

    for step in steps:
        sum_piece(step).start()
    out_copies[-1].start()
    for step in steps:
        sum_piece(step).wait()
    for step in steps:
        total = total + gathered[step - 1]
    noise_ref[...] = total / (PULSES * gates) + epsilon
    for copy in out_copies:
        copy.wait()


def fused(sections, subs, echoes, range_taps, pulse_taper, channel_phase, loading, beam_index):
    parts = sections * subs
    local_gates, local_channels = echoes.shape[2:]
    gates, channels = local_gates * sections, local_channels * subs
    bins = PULSES // parts
    beam_count = beam_index.shape[0]
    units = INTERVALS * bins // BLOCK
    width = local_gates * local_channels
    flat = echoes.reshape(2 * echoes.shape[1] * local_gates, local_channels)
    vmem = pl.BlockSpec(memory_space=pltpu.VMEM)
    smem = pl.BlockSpec(memory_space=pltpu.SMEM)
    whole = pl.BlockSpec(memory_space=pl.ANY)
    power, noise_level = pl.pallas_call(
        functools.partial(kernel, sections, subs, gates, channels, bins),
        out_shape=(
            jax.ShapeDtypeStruct((bins, gates, beam_count), f32),
            jax.ShapeDtypeStruct((1, beam_count), f32),
        ),
        in_specs=[whole] * 2 + [vmem] * 3 + [smem] * 2,
        out_specs=(whole, vmem),
        scratch_shapes=[
            pltpu.VMEM(flat.shape, f32),
            pltpu.VMEM((2 * PULSES, 2 * PULSES), f32),
            pltpu.VMEM((2 * PULSES, 2 * PULSES), bf16),
            pltpu.VMEM((2 * PULSES, 2 * PULSES), bf16),
            pltpu.VMEM((2 * channels, 2 * beam_count), bf16),
            pltpu.VMEM((2 * channels, 2 * beam_count), bf16),
            pltpu.VMEM((units, parts * 2 * BLOCK, width), f32),
            pltpu.VMEM((units, parts + 2 * subs, 2 * BLOCK, width), f32),
            pltpu.VMEM((subs, 2 * gates * BLOCK, local_channels), f32),
            pltpu.VMEM((beam_count // 128, 2 * gates * BLOCK, 128), f32),
            pltpu.VMEM((bins, 2 * gates, 2 * channels), bf16),
            pltpu.VMEM((bins, 2 * gates, 2 * channels), bf16),
            pltpu.VMEM((bins, 2 * gates, beam_count), bf16),
            pltpu.VMEM((bins, 2 * gates, beam_count), bf16),
            pltpu.VMEM((bins, 1, beam_count), f32),
            pltpu.VMEM((bins, gates, beam_count), f32),
            pltpu.VMEM((1, beam_count), f32),
            pltpu.VMEM((parts - 1, 1, beam_count), f32),
            pltpu.SemaphoreType.DMA((4,)),
            pltpu.SemaphoreType.DMA,
            pltpu.SemaphoreType.DMA((units, parts - 1)),
            pltpu.SemaphoreType.DMA((units, parts - 1)),
            pltpu.SemaphoreType.DMA((units,)),
            pltpu.SemaphoreType.DMA((parts - 1,)),
            pltpu.SemaphoreType.DMA((parts - 1,)),
            pltpu.SemaphoreType.DMA((bins // BLOCK,)),
        ],
        compiler_params=pltpu.CompilerParams(
            collective_id=0, has_side_effects=True, vmem_limit_bytes=56 * 2**20
        ),
        name="beams",
    )(
        flat, jnp.asarray(fourier_rows(parts)), pulse_taper[None, :], channel_phase[None, :], beam_index[None, :],
        range_taps, loading,
    )
    return (power / noise_level)[None]


def solution(mesh):
    sections, subs = mesh.shape["section"], mesh.shape["sub"]
    parts = sections * subs

    def body(echoes, *rest):
        local_gates, local_channels = echoes.shape[2:]
        gates, channels = local_gates * sections, local_channels * subs
        fits = (
            parts & (parts - 1) == 0
            and PULSES % parts == 0
            and (PULSES // parts) % BLOCK == 0
            and echoes.shape[1] == (INTERVALS - 1) * HOP + PULSES
            and INTERVALS == 2
            and ITERS == 2
            and gates % 8 == 0
            and 2 * gates <= channels
            and local_channels == 128
            and rest[-1].shape[0] % 128 == 0
            and local_gates >= rest[0].shape[1] // 2
            and channels == rest[-1].shape[0]
        )
        if fits:
            return fused(sections, subs, echoes, *rest)
        return on_device(echoes, *rest)

    in_specs = (P("groups", None, "section", "sub"), P(), P(), P(), P(), P())
    out_specs = P("groups", ("section", "sub"), None, None)
    return jax.shard_map(
        body, mesh=mesh, in_specs=in_specs, out_specs=out_specs, check_vma=False
    )
```
